32 devices in a mesh: sec: 2 (over x), tile: 16 (over z, y, core).
Axes of the slice: x: 2, y: 2, z: 4, core: 2. Of those that a mesh axis runs over, the one named last changes fastest.
Arguments:
- start_modes: bfloat16 [16, 24, 384, 384], P('sec', None, 'tile'), may hold values from -6 to 6
- permittivity: bfloat16 [16, 384, 384], P('sec', 'tile'), may hold values from 1 to 12
- heights: int32 [16], replicated, may hold values from 192 to 384, as said below
Outputs:
- mode_fields: bfloat16 [16, 24, 384, 384], P('sec', None, 'tile')
- coupling: float32 [16, 24, 24], P('sec')
The draws below stay inside these ranges and needn't reach their ends.
Inputs may be any that keep to these rules, and one draw needn't show every extreme that they name: heights[s] is the number of rows in use of section s, counted from row 0; some section uses all 384 rows.
All inputs are finite; a program needn't handle non-finite values.
Results may differ from the reference program's by a relative error of at most 0.001.
Values may be sent and summed in bfloat16 or wider, within the bound.
A program may use at most 128 MiB of HBM per device.

```python
import math
import jax
import jax.numpy as jnp
from jax import lax

M = 24
GC = 384
GR = 384
STEPS = 3
DEG = 4
SECTIONS = 16


def draw_heights(key, part):
    first, second = jax.random.split(jax.random.fold_in(key, 11))
    drawn = jax.random.randint(first, (SECTIONS,), GR // 2, GR + 1)
    chosen = jax.random.randint(second, (), 0, SECTIONS)
    return jnp.where(jnp.arange(SECTIONS) == chosen, GR, drawn).astype(jnp.int32)


def block_scale(stream_key, shape, pieces, least, largest):
    factor_of, own = 1.0, jax.random.fold_in(stream_key, 6)
    for position, shards_of in pieces:
        steps = jnp.exp(jax.random.uniform(jax.random.fold_in(own, position), (shards_of,), jnp.float32, least / len(pieces), largest / len(pieces)))
        factor_of = factor_of * jnp.repeat(steps, shape[position] // shards_of).reshape([-1 if axis == position else 1 for axis in range(len(shape))])
    return factor_of


def scatter_about(key, extent, width, most, cuts=(), kind=jnp.bfloat16):
    level = block_scale(key, extent, cuts, -0.22, 0.18) if cuts else 1.0
    values = jax.random.normal(key, extent, jnp.float32) * width * level
    return jnp.minimum(jnp.maximum(values, -most), most).astype(kind)


def setup_inputs(seed: int = 0) -> dict:
    seeds = jax.random.split(jax.random.key(seed), 4)
    start_modes = scatter_about(seeds[0], (SECTIONS, M, GR, GC), 1.0, 6.0, ((0, 2), (2, 16)))
    permittivity = jnp.clip(jnp.exp(math.log(12.0) - 2.4849066 * jax.random.uniform(seeds[1], (SECTIONS, GR, GC), jnp.float32) ** block_scale(seeds[1], (SECTIONS, GR, GC), ((0, 2), (1, 16)), -0.2, 0.2)), 1.0, 12.0).astype(jnp.bfloat16)
    heights = draw_heights(jax.random.fold_in(seeds[3], 71), 0)
    return {"start_modes": start_modes, "permittivity": permittivity, "heights": heights}


SHIFT_DIAG = 3.0
EPS_WEIGHT = 0.25
LOWER_EDGE = 2.0
UPPER_EDGE = 10.75

def chebyshev_terms(degree):
    center = 0.5 * (UPPER_EDGE + LOWER_EDGE)
    radius = 0.5 * (UPPER_EDGE - LOWER_EDGE)
    anchor = -center / radius
    values = [1.0, anchor]
    for order in range(1, degree):
        values.append(2.0 * anchor * values[order] - values[order - 1])
    return (center, radius, values)

def scaled_apply(padded, field, diag_scaled, row_mask, inverse):
    sided = jnp.pad(field, ((0, 0), (0, 0), (0, 0), (1, 1)))
    beside = padded[:, :, 2:, :] + padded[:, :, :-2, :] + sided[:, :, :, 2:] + sided[:, :, :, :-2]
    return (diag_scaled * field - inverse * beside) * row_mask

def filter_steps(field, apply_once, degree):
    center, radius, values = chebyshev_terms(degree)
    previous = field
    current = apply_once(field) * (1.0 / values[1])
    for order in range(1, degree):
        upcoming = apply_once(current) * (2.0 * values[order] / values[order + 1]) - previous * (values[order - 1] / values[order + 1])
        previous = current
        current = upcoming
    return current

def orthonormal(field):
    gram = jnp.einsum('smrc,snrc->smn', field, field, precision=lax.Precision.HIGHEST)
    lower = jnp.linalg.cholesky(gram)
    flat = field.reshape(field.shape[0], field.shape[1], -1)
    solved = lax.linalg.triangular_solve(lower, flat, left_side=True, lower=True)
    return solved.reshape(field.shape)

def reference(start_modes, permittivity, heights):
    center, radius, values = chebyshev_terms(DEG)
    inverse = 1.0 / radius
    row_ids = jnp.arange(GR, dtype=jnp.int32)

    def one_section(packed):
        start, perm, height = packed
        row_mask = (row_ids < height).astype(jnp.float32)[None, None, :, None]
        diag_scaled = ((4.0 + SHIFT_DIAG - EPS_WEIGHT * perm.astype(jnp.float32) - center) * inverse)[None, None]

        def apply_once(current):
            padded = jnp.pad(current, ((0, 0), (0, 0), (1, 1), (0, 0)))
            return scaled_apply(padded, current, diag_scaled, row_mask, inverse)
        field = start.astype(jnp.float32)[None] * row_mask
        for step in range(STEPS):
            field = orthonormal(filter_steps(field, apply_once, DEG))
        return (field[0] * GC).astype(jnp.bfloat16)
    mode_fields = lax.map(one_section, (start_modes, permittivity, heights))
    following = jnp.concatenate([mode_fields[1:], jnp.zeros_like(mode_fields[:1])], 0)

    def pair(packed):
        here, there = packed
        return jnp.dot(here.reshape(M, -1).astype(jnp.float32), there.reshape(M, -1).T.astype(jnp.float32), preferred_element_type=jnp.float32)
    coupling = lax.map(pair, (mode_fields, following)) / (GC * math.sqrt(GC))
    return (mode_fields, coupling)
```

```python
import functools
import math

import jax
import jax.numpy as jnp
from jax import lax
from jax.experimental import pallas as pl
from jax.experimental.pallas import tpu as pltpu
from jax.sharding import PartitionSpec as P

STEPS = 3
DEG = 4
SHIFT_DIAG = 3.0
EPS_WEIGHT = 0.25
LOWER_EDGE = 2.0
UPPER_EDGE = 10.75
CENTER = 0.5 * (UPPER_EDGE + LOWER_EDGE)
RADIUS = 0.5 * (UPPER_EDGE - LOWER_EDGE)
LANES = 128
SLOT = 32
PER = LANES // SLOT
BLOCK = 4
NT = (((1,), (1,)), ((), ()))
MESH = pl.DeviceIdType.MESH


def iota(shape, dim):
    return lax.broadcasted_iota(jnp.int32, shape, dim)


def dot32(a, b):
    return jnp.dot(a, b, preferred_element_type=jnp.float32)


def dot_nt(a, b):
    return lax.dot_general(a, b, NT, preferred_element_type=jnp.float32)


def halo(x, dim, width):
    size, strip = lax.axis_size("tile"), x.shape[dim]
    above, below = [], []
    for hop in range(1, -(-width // strip) + 1):
        rows = min(strip, width - (hop - 1) * strip)
        last = lax.slice_in_dim(x, strip - rows, strip, axis=dim)
        first = lax.slice_in_dim(x, 0, rows, axis=dim)
        above.insert(0, lax.ppermute(last, "tile", [(i, i + hop) for i in range(size - hop)]))
        below.append(lax.ppermute(first, "tile", [(i + hop, i) for i in range(size - hop)]))
    return above, below


def widened(x, dim, width, total):
    above, below = halo(x, dim, width)
    spare = total - x.shape[dim] - 2 * width
    parts = above + [x] + below
    if spare:
        shape = list(x.shape)
        shape[dim] = spare
        parts.append(jnp.zeros(shape, x.dtype))
    return jnp.concatenate(parts, axis=dim)


def interleave(columns, groups, inverse=False):
    row, col = iota((columns, columns), 0), iota((columns, columns), 1)
    if inverse:
        row, col = col, row
    return (row == groups * (col % LANES) + col // LANES).astype(jnp.bfloat16)


def place(small, wide_ref, out_ref, s, modes):
    wide_ref[:, 0:modes] = small
    moved = pltpu.roll(wide_ref[...], SLOT * lax.rem(s, PER), 1)
    group = s // PER
    out_ref[group] = out_ref[group] + moved


def filter_kernel(strip, heights, x_ref, perm_ref, field_ref, gram_ref, a_ref, b_ref, q_ref, mix_ref, high_ref, low_ref, wide_ref):
    modes, rows, columns = x_ref.shape[1:]
    groups = columns // LANES
    width = STEPS * DEG
    used = strip + 2 * width
    s = pl.program_id(0)
    sections = pl.num_programs(0)
    height = heights[lax.axis_index("sec") * sections + s]
    top = lax.axis_index("tile") * strip - width

    @pl.when(s == 0)
    def _():
        mix_ref[...] = interleave(columns, groups)
        a_ref[...] = jnp.zeros_like(a_ref)
        b_ref[...] = jnp.zeros_like(b_ref)
        wide_ref[...] = jnp.zeros_like(wide_ref)
        gram_ref[...] = jnp.zeros_like(gram_ref)

    mix = mix_ref[...]
    row_ids = top + iota((rows, LANES), 0)
    valid = (row_ids >= 0) & (row_ids < height)
    batch = 4
    for m0 in range(0, modes, batch):
        moved = dot32(x_ref[0, m0 : m0 + batch].reshape(batch * rows, columns), mix)
        for m in range(batch):
            for j in range(groups):
                value = moved[m * rows : (m + 1) * rows, j * LANES : (j + 1) * LANES]
                a_ref[j, pl.ds(modes + m0 + m, rows, stride=modes), :] = jnp.where(valid, value, 0.0)
    perm = dot32(perm_ref[0], mix)
    diag = (4.0 + SHIFT_DIAG - EPS_WEIGHT * perm - CENTER) * (2.0 / RADIUS)
    for j in range(groups):
        q_ref[j] = diag[:, j * LANES : (j + 1) * LANES]

    lane = iota((8, LANES), 1)
    is_first, is_last = lane == 0, lane == LANES - 1

    def stage(src, dst, order, start):
        low = BLOCK * (order // BLOCK)
        blocks = -(-(used - order - low) // BLOCK)

        def body(block, carry):
            row0 = low + block * BLOCK
            base = pl.multiple_of((row0 + 1) * modes, 8)
            for tile in range(modes // 8):
                def load(ref, i, j):
                    return ref[j, pl.ds(pl.multiple_of(base + (i * modes + tile * 8), 8), 8), :]

                before = [load(src, -1, j) for j in range(groups)]
                here = [load(src, 0, j) for j in range(groups)]
                for i in range(BLOCK):
                    after = [load(src, i + 1, j) for j in range(groups)]
                    row = top + row0 + i
                    inside = (row >= 0) & (row < height)
                    weight = jnp.where(inside, 2.0 / RADIUS, 0.0).astype(jnp.float32)
                    left = jnp.where(is_first, 0.0, pltpu.roll(here[groups - 1], 1, 1))
                    right = jnp.where(is_last, 0.0, pltpu.roll(here[0], LANES - 1, 1))
                    for j in range(groups):
                        side = (here[j - 1] if j else left) + (here[j + 1] if j < groups - 1 else right)
                        beside = (before[j] + after[j]) + side
                        q = jnp.broadcast_to(q_ref[j, pl.ds(row0 + i, 1), :], (8, LANES))
                        value = q * here[j] - weight * beside
                        if start:
                            value = 0.5 * value
                        else:
                            value = value - load(dst, i, j)
                        dst[j, pl.ds(pl.multiple_of(base + (i * modes + tile * 8), 8), 8), :] = value
                    before, here = here, after
            return carry

        lax.fori_loop(0, blocks, body, 0)

    for step in range(STEPS):
        for k in range(DEG):
            src, dst = (a_ref, b_ref) if k % 2 == 0 else (b_ref, a_ref)
            stage(src, dst, step * DEG + k + 1, k == 0)

    for j in range(groups):
        field_ref[0, j] = a_ref[j, (width + 1) * modes : (width + 1 + strip) * modes, :]
    for r in range(strip):
        for j in range(groups):
            value = a_ref[j, (width + 1 + r) * modes : (width + 2 + r) * modes, :]
            high = value.astype(jnp.bfloat16)
            place_at = slice((r * groups + j) * LANES, (r * groups + j + 1) * LANES)
            high_ref[:, place_at] = high
            low_ref[:, place_at] = (value - high.astype(jnp.float32)).astype(jnp.bfloat16)
    high, low = high_ref[...], low_ref[...]
    gram = dot_nt(high, high) + (dot_nt(high, low) + dot_nt(low, high))
    place(gram, wide_ref, gram_ref, s, modes)


def gathered_sum(x_ref, slots, send_sem, recv_sem):
    count = lax.axis_size("tile")
    me = lax.axis_index("tile")
    barrier = pltpu.get_barrier_semaphore()

    def greet(d, carry):
        pl.semaphore_signal(barrier, inc=1, device_id={"tile": lax.rem(me + d, count)}, device_id_type=MESH)
        return carry

    lax.fori_loop(1, count, greet, 0)
    pl.semaphore_wait(barrier, count - 1)

    def copy_to(d, slot):
        return pltpu.make_async_remote_copy(
            src_ref=x_ref,
            dst_ref=slots.at[slot],
            send_sem=send_sem.at[d],
            recv_sem=recv_sem.at[slot],
            device_id={"tile": lax.rem(me + d, count)},
            device_id_type=MESH,
        )

    def send(d, carry):
        copy_to(d, me).start()
        return carry

    def finish(d, carry):
        copy_to(d, lax.rem(me + count - d, count)).wait_recv()
        copy_to(d, me).wait_send()
        return carry

    lax.fori_loop(1, count, send, 0)
    slots[me] = x_ref[...]
    lax.fori_loop(1, count, finish, 0)
    return lax.fori_loop(1, count, lambda i, total: total + slots[i], slots[0])


def spread(total, sections):
    return jnp.stack([pltpu.roll(total[s // PER], (LANES - SLOT * (s % PER)) % LANES, 1) if s % PER else total[s // PER] for s in range(sections)])


def factor_kernel(scale, x_ref, out_ref, slots, send_sem, recv_sem):
    sections, modes, _ = out_ref.shape
    total = gathered_sum(x_ref, slots, send_sem, recv_sem)
    shape = (sections, modes, LANES)
    row, lane = iota(shape, 1), iota(shape, 2)
    work = jnp.where(lane < modes, spread(total, sections), jnp.where(lane == row + SLOT, 1.0, 0.0))
    for k in range(modes):
        top = work[:, k : k + 1, :]
        pivot = jnp.sqrt(work[:, k : k + 1, k : k + 1])
        top = top / pivot
        column = work[:, :, k : k + 1] / pivot
        work = jnp.where(row > k, work - column * top, jnp.where(row == k, top, work))
    for s in range(sections):
        moved = pltpu.roll(work[s], LANES - SLOT, 1)
        out_ref[s] = moved[:, 0:modes] * scale


def apply_kernel(strip, inv_ref, field_ref, out_ref, first_ref, last_ref, pack_ref, unmix_ref, both_ref, rows_ref, wide_ref):
    modes = inv_ref.shape[1]
    groups = field_ref.shape[1]
    columns = groups * LANES
    s = pl.program_id(0)
    take = max(n for n in range(1, 9) if strip % n == 0)
    size = take * modes

    @pl.when(s == 0)
    def _():
        unmix_ref[...] = interleave(columns, groups, True)
        wide_ref[...] = jnp.zeros_like(wide_ref)
        pack_ref[...] = jnp.zeros_like(pack_ref)

    copies = (iota((size, modes), 0) % modes == iota((size, modes), 1)).astype(jnp.bfloat16)
    same = iota((size, size), 0) // modes == iota((size, size), 1) // modes

    def block_diagonal(part):
        tall = dot32(copies, part).astype(jnp.bfloat16)
        return jnp.where(same, dot_nt(tall, copies), 0.0).astype(jnp.bfloat16)

    inv = inv_ref[0]
    inv_high = inv.astype(jnp.bfloat16)
    inv_low = (inv - inv_high.astype(jnp.float32)).astype(jnp.bfloat16)
    left_high, left_low = block_diagonal(inv_high), block_diagonal(inv_low)
    unmix = unmix_ref[...]
    slot = lax.rem(s, 2)
    for r0 in range(0, strip, take):
        value = jnp.concatenate([field_ref[0, j, r0 * modes : r0 * modes + size, :] for j in range(groups)], axis=1)
        high = value.astype(jnp.bfloat16)
        low = (value - high.astype(jnp.float32)).astype(jnp.bfloat16)
        solved = dot32(left_high, high) + (dot32(left_low, high) + dot32(left_high, low))
        for r in range(take):
            both_ref[slot, :, (r0 + r) * columns : (r0 + r + 1) * columns] = solved[r * modes : (r + 1) * modes].astype(jnp.bfloat16)
        natural = dot32(solved.astype(jnp.bfloat16), unmix)
        for j in range(groups):
            rows_ref[j, r0 * modes : r0 * modes + size, :] = natural[:, j * LANES : (j + 1) * LANES]
    for m in range(modes):
        for j in range(groups):
            out_ref[0, m, :, j * LANES : (j + 1) * LANES] = rows_ref[j, pl.ds(m, strip, stride=modes), :].astype(jnp.bfloat16)

    @pl.when(s == 0)
    def _():
        first_ref[...] = both_ref[slot]

    @pl.when(s > 0)
    def _():
        place(dot_nt(both_ref[1 - slot], both_ref[slot]), wide_ref, pack_ref, s - 1, modes)

    @pl.when(s == pl.num_programs(0) - 1)
    def _():
        last_ref[...] = both_ref[slot]


def edge_kernel(sections, pack_ref, last_ref, next_ref, out_ref, wide_ref):
    wide_ref[...] = jnp.zeros_like(wide_ref)
    out_ref[...] = pack_ref[...]
    place(dot_nt(last_ref[...], next_ref[...]), wide_ref, out_ref, jnp.int32(sections - 1), last_ref.shape[0])


def couple_kernel(columns, x_ref, out_ref, slots, send_sem, recv_sem):
    sections, modes, _ = out_ref.shape
    total = gathered_sum(x_ref, slots, send_sem, recv_sem)
    parts = spread(total, sections)
    end = lax.axis_size("sec") * sections - 1
    for s in range(sections):
        kept = jnp.where(lax.axis_index("sec") * sections + s < end, 1.0 / (columns * math.sqrt(columns)), 0.0)
        out_ref[s] = parts[s][:, 0:modes] * kept.astype(jnp.float32)


def per_device(start_modes, permittivity, heights):
    sections, modes, strip, columns = start_modes.shape
    groups = columns // LANES
    width = STEPS * DEG
    rows = -(-(strip + 2 * width) // 16) * 16
    packs = -(-sections // PER)
    tiles = lax.axis_size("tile")
    f32, bf16 = jnp.float32, jnp.bfloat16
    x = widened(start_modes, 2, width, rows)
    perm = widened(permittivity, 1, width, rows)
    pack_shape = jax.ShapeDtypeStruct((packs, modes, LANES), f32)
    pack_spec = pl.BlockSpec((packs, modes, LANES), lambda s, *_: (0, 0, 0))
    field_spec = pl.BlockSpec((1, groups, strip * modes, LANES), lambda s, *_: (s, 0, 0, 0))
    field, gram = pl.pallas_call(
        functools.partial(filter_kernel, strip),
        grid_spec=pltpu.PrefetchScalarGridSpec(
            num_scalar_prefetch=1,
            grid=(sections,),
            in_specs=[
                pl.BlockSpec((1, modes, rows, columns), lambda s, *_: (s, 0, 0, 0)),
                pl.BlockSpec((1, rows, columns), lambda s, *_: (s, 0, 0)),
            ],
            out_specs=[field_spec, pack_spec],
            scratch_shapes=[
                pltpu.VMEM((groups, (rows + 2) * modes, LANES), f32),
                pltpu.VMEM((groups, (rows + 2) * modes, LANES), f32),
                pltpu.VMEM((groups, rows, LANES), f32),
                pltpu.VMEM((columns, columns), bf16),
                pltpu.VMEM((modes, strip * columns), bf16),
                pltpu.VMEM((modes, strip * columns), bf16),
                pltpu.VMEM((modes, LANES), f32),
            ],
        ),
        out_shape=[jax.ShapeDtypeStruct((sections, groups, strip * modes, LANES), f32), pack_shape],
        name="filter",
    )(heights, x, perm)

    def exchanged(kernel, value, collective_id, name):
        return pl.pallas_call(
            kernel,
            out_shape=jax.ShapeDtypeStruct((sections, modes, modes), f32),
            in_specs=[pl.BlockSpec(memory_space=pltpu.VMEM)],
            out_specs=pl.BlockSpec(memory_space=pltpu.VMEM),
            scratch_shapes=[
                pltpu.VMEM((tiles, packs, modes, LANES), f32),
                pltpu.SemaphoreType.DMA((tiles,)),
                pltpu.SemaphoreType.DMA((tiles,)),
            ],
            compiler_params=pltpu.CompilerParams(collective_id=collective_id, has_side_effects=True),
            name=name,
        )(value)

    inverse = exchanged(functools.partial(factor_kernel, float(columns)), gram, 0, "factor")
    flat = jax.ShapeDtypeStruct((modes, strip * columns), bf16)
    flat_spec = pl.BlockSpec((modes, strip * columns), lambda s: (0, 0))
    scaled, first, last, pack = pl.pallas_call(
        functools.partial(apply_kernel, strip),
        grid=(sections,),
        in_specs=[pl.BlockSpec((1, modes, modes), lambda s: (s, 0, 0)), field_spec],
        out_specs=[pl.BlockSpec((1, modes, strip, columns), lambda s: (s, 0, 0, 0)), flat_spec, flat_spec, pack_spec],
        out_shape=[jax.ShapeDtypeStruct((sections, modes, strip, columns), bf16), flat, flat, pack_shape],
        scratch_shapes=[
            pltpu.VMEM((columns, columns), bf16),
            pltpu.VMEM((2, modes, strip * columns), bf16),
            pltpu.VMEM((groups, strip * modes, LANES), f32),
            pltpu.VMEM((modes, LANES), f32),
        ],
        name="apply",
    )(inverse, field)
    count = lax.axis_size("sec")
    arriving = lax.ppermute(first, "sec", [(i + 1, i) for i in range(count - 1)])
    pack = pl.pallas_call(
        functools.partial(edge_kernel, sections),
        out_shape=pack_shape,
        scratch_shapes=[pltpu.VMEM((modes, LANES), f32)],
        name="edge",
    )(pack, last, arriving)
    coupling = exchanged(functools.partial(couple_kernel, columns), pack, 1, "couple")
    return (scaled, coupling)


def solution(mesh):
    placed = (P("sec", None, "tile", None), P("sec", "tile", None), P())
    return jax.shard_map(
        per_device,
        mesh=mesh,
        in_specs=placed,
        out_specs=(P("sec", None, "tile", None), P("sec", None, None)),
        check_vma=False,
    )
```

```python
import functools
import math

import jax
import jax.numpy as jnp
from jax import lax
from jax.experimental import pallas as pl
from jax.experimental.pallas import tpu as pltpu
from jax.sharding import PartitionSpec as P

STEPS = 3
DEG = 4
SHIFT_DIAG = 3.0
EPS_WEIGHT = 0.25
LOWER_EDGE = 2.0
UPPER_EDGE = 10.75
CENTER = 0.5 * (UPPER_EDGE + LOWER_EDGE)
RADIUS = 0.5 * (UPPER_EDGE - LOWER_EDGE)
LANES = 128
SLOT = 32
PER = LANES // SLOT
BLOCK = 8

NT = (((1,), (1,)), ((), ()))
MESH = pl.DeviceIdType.MESH


def iota(shape, dim):
    return lax.broadcasted_iota(jnp.int32, shape, dim)


def dot32(a, b):
    return jnp.dot(a, b, preferred_element_type=jnp.float32)


def dot_nt(a, b):
    return lax.dot_general(a, b, NT, preferred_element_type=jnp.float32)


def halo(x, dim, width):
    size, strip = lax.axis_size("tile"), x.shape[dim]
    above, below = [], []
    for hop in range(1, -(-width // strip) + 1):
        rows = min(strip, width - (hop - 1) * strip)
        last = lax.slice_in_dim(x, strip - rows, strip, axis=dim)
        first = lax.slice_in_dim(x, 0, rows, axis=dim)
        above.insert(0, lax.ppermute(last, "tile", [(i, i + hop) for i in range(size - hop)]))
        below.append(lax.ppermute(first, "tile", [(i + hop, i) for i in range(size - hop)]))
    return above, below


def widened(x, dim, width, total):
    above, below = halo(x, dim, width)
    spare = total - x.shape[dim] - 2 * width
    parts = above + [x] + below
    if spare:
        shape = list(x.shape)
        shape[dim] = spare
        parts.append(jnp.zeros(shape, x.dtype))
    return jnp.concatenate(parts, axis=dim)


def interleave(columns, groups, inverse=False):
    row, col = iota((columns, columns), 0), iota((columns, columns), 1)
    if inverse:
        row, col = col, row
    return (row == groups * (col % LANES) + col // LANES).astype(jnp.bfloat16)


def place(small, wide_ref, out_ref, s, modes):
    wide_ref[:, 0:modes] = small
    moved = pltpu.roll(wide_ref[...], SLOT * lax.rem(s, PER), 1)
    group = s // PER
    out_ref[group] = out_ref[group] + moved


def filter_kernel(strip, section0, sections, heights, x_ref, perm_ref, whole_ref, field_ref, gram_ref, a_ref, b_ref, q_ref, mix_ref, high_ref, low_ref, wide_ref):
    modes, rows, columns = x_ref.shape[1:]
    groups = columns // LANES
    width = STEPS * DEG
    used = strip + 2 * width
    s = pl.program_id(0)
    height = heights[lax.axis_index("sec") * sections + section0 + s]
    top = lax.axis_index("tile") * strip - width

    @pl.when(s == 0)
    def _():
        mix_ref[...] = interleave(columns, groups)
        a_ref[...] = jnp.zeros_like(a_ref)
        b_ref[...] = jnp.zeros_like(b_ref)
        wide_ref[...] = jnp.zeros_like(wide_ref)
        gram_ref[...] = jnp.zeros_like(gram_ref)

    mix = mix_ref[...]
    row_ids = top + iota((rows, LANES), 0)
    valid = (row_ids >= 0) & (row_ids < height)
    batch = 4
    for m0 in range(0, modes, batch):
        moved = dot32(x_ref[0, m0 : m0 + batch].reshape(batch * rows, columns), mix)
        for m in range(batch):
            for j in range(groups):
                value = moved[m * rows : (m + 1) * rows, j * LANES : (j + 1) * LANES]
                a_ref[j, pl.ds(modes + m0 + m, rows, stride=modes), :] = jnp.where(valid, value, 0.0)
    perm = dot32(perm_ref[0], mix)
    diag = (4.0 + SHIFT_DIAG - EPS_WEIGHT * perm - CENTER) * (2.0 / RADIUS)
    for j in range(groups):
        q_ref[j] = diag[:, j * LANES : (j + 1) * LANES]

    lane = iota((8, LANES), 1)
    is_first, is_last = lane == 0, lane == LANES - 1

    def stage(src, dst, order, start):
        blocks = -(-(used - 2 * order) // BLOCK)
        low = min(order, rows - blocks * BLOCK)

        def body(block, carry):
            row0 = low + block * BLOCK
            base = pl.multiple_of((row0 + 1) * modes, 8)
            for tile in range(modes // 8):
                def load(ref, i, j):
                    return ref[j, pl.ds(pl.multiple_of(base + (i * modes + tile * 8), 8), 8), :]

                before = [load(src, -1, j) for j in range(groups)]
                here = [load(src, 0, j) for j in range(groups)]
                for i in range(BLOCK):
                    after = [load(src, i + 1, j) for j in range(groups)]
                    row = top + row0 + i
                    inside = (row >= 0) & (row < height)
                    weight = jnp.where(inside, 2.0 / RADIUS, 0.0).astype(jnp.float32)
                    left = jnp.where(is_first, 0.0, pltpu.roll(here[groups - 1], 1, 1))
                    right = jnp.where(is_last, 0.0, pltpu.roll(here[0], LANES - 1, 1))
                    for j in range(groups):
                        side = (here[j - 1] if j else left) + (here[j + 1] if j < groups - 1 else right)
                        beside = (before[j] + after[j]) + side
                        q = jnp.broadcast_to(q_ref[j, pl.ds(row0 + i, 1), :], (8, LANES))
                        value = q * here[j] - weight * beside
                        if start:
                            value = 0.5 * value
                        else:
                            value = value - load(dst, i, j)
                        dst[j, pl.ds(pl.multiple_of(base + (i * modes + tile * 8), 8), 8), :] = value
                    before, here = here, after
            return carry

        lax.fori_loop(0, blocks, body, 0)

    for step in range(STEPS):
        for k in range(DEG):
            src, dst = (a_ref, b_ref) if k % 2 == 0 else (b_ref, a_ref)
            stage(src, dst, step * DEG + k + 1, k == 0)

    for j in range(groups):
        field_ref[0, j] = a_ref[j, (width + 1) * modes : (width + 1 + strip) * modes, :]
    for r in range(strip):
        for j in range(groups):
            value = a_ref[j, (width + 1 + r) * modes : (width + 2 + r) * modes, :]
            high = value.astype(jnp.bfloat16)
            place_at = slice((r * groups + j) * LANES, (r * groups + j + 1) * LANES)
            high_ref[:, place_at] = high
            low_ref[:, place_at] = (value - high.astype(jnp.float32)).astype(jnp.bfloat16)
    high, low = high_ref[...], low_ref[...]
    gram = dot_nt(high, high) + (dot_nt(high, low) + dot_nt(low, high))
    place(gram, wide_ref, gram_ref, s, modes)


def gathered_sum(x_ref, slots, send_sem, recv_sem):
    count = lax.axis_size("tile")
    me = lax.axis_index("tile")
    barrier = pltpu.get_barrier_semaphore()

    def greet(d, carry):
        pl.semaphore_signal(barrier, inc=1, device_id={"tile": lax.rem(me + d, count)}, device_id_type=MESH)
        return carry

    lax.fori_loop(1, count, greet, 0)
    pl.semaphore_wait(barrier, count - 1)

    def copy_to(d, slot):
        return pltpu.make_async_remote_copy(
            src_ref=x_ref,
            dst_ref=slots.at[slot],
            send_sem=send_sem.at[d],
            recv_sem=recv_sem.at[slot],
            device_id={"tile": lax.rem(me + d, count)},
            device_id_type=MESH,
        )

    def send(d, carry):
        copy_to(d, me).start()
        return carry

    def finish(d, carry):
        copy_to(d, lax.rem(me + count - d, count)).wait_recv()
        copy_to(d, me).wait_send()
        return carry

    lax.fori_loop(1, count, send, 0)
    slots[me] = x_ref[...]
    lax.fori_loop(1, count, finish, 0)
    return lax.fori_loop(1, count, lambda i, total: total + slots[i], slots[0])


def spread(total, sections):
    return jnp.stack([pltpu.roll(total[s // PER], (LANES - SLOT * (s % PER)) % LANES, 1) if s % PER else total[s // PER] for s in range(sections)])


def factor_kernel(scale, x_ref, out_ref, slots, send_sem, recv_sem):
    sections, modes, _ = out_ref.shape
    total = gathered_sum(x_ref, slots, send_sem, recv_sem)
    shape = (sections, modes, LANES)
    row, lane = iota(shape, 1), iota(shape, 2)
    work = jnp.where(lane < modes, spread(total, sections), jnp.where(lane == row + SLOT, 1.0, 0.0))
    pivots = jnp.ones((sections, modes, 1), jnp.float32)
    for k in range(modes):
        top = work[:, k : k + 1, :]
        pivot = work[:, k : k + 1, k : k + 1]
        pivots = jnp.where(row[:, :, 0:1] == k, pivot, pivots)
        if k < modes - 1:
            column = jnp.where(row > k, work[:, :, k : k + 1], 0.0)
            work = work - column * (top * (1.0 / pivot))
    work = work * (scale / jnp.sqrt(pivots))
    for s in range(sections):
        moved = pltpu.roll(work[s], LANES - SLOT, 1)
        out_ref[s] = moved[:, 0:modes]


def apply_section(strip, inv_ref, field_ref, out_ref, unmix_ref, both_ref, rows_ref, slot):
    modes = inv_ref.shape[1]
    groups = field_ref.shape[1]
    columns = groups * LANES
    take = max(n for n in range(1, 9) if strip % n == 0)
    size = take * modes


    @pl.when(pl.program_id(0) == 0)
    def _():
        unmix_ref[...] = interleave(columns, groups, True)

    copies = (iota((size, modes), 0) % modes == iota((size, modes), 1)).astype(jnp.bfloat16)
    same = iota((size, size), 0) // modes == iota((size, size), 1) // modes

    def block_diagonal(part):
        tall = dot32(copies, part).astype(jnp.bfloat16)
        return jnp.where(same, dot_nt(tall, copies), 0.0).astype(jnp.bfloat16)

    inv = inv_ref[0]
    inv_high = inv.astype(jnp.bfloat16)
    inv_low = (inv - inv_high.astype(jnp.float32)).astype(jnp.bfloat16)
    left_high, left_low = block_diagonal(inv_high), block_diagonal(inv_low)
    unmix = unmix_ref[...]
    for r0 in range(0, strip, take):
        value = jnp.concatenate([field_ref[0, j, r0 * modes : r0 * modes + size, :] for j in range(groups)], axis=1)
        high = value.astype(jnp.bfloat16)
        low = (value - high.astype(jnp.float32)).astype(jnp.bfloat16)
        solved = dot32(left_high, high) + (dot32(left_low, high) + dot32(left_high, low))
        for r in range(take):
            both_ref[slot, :, (r0 + r) * columns : (r0 + r + 1) * columns] = solved[r * modes : (r + 1) * modes].astype(jnp.bfloat16)
        natural = dot32(solved.astype(jnp.bfloat16), unmix)
        for j in range(groups):
            rows_ref[j, r0 * modes : r0 * modes + size, :] = natural[:, j * LANES : (j + 1) * LANES]
    for m in range(modes):
        for j in range(groups):
            out_ref[0, m, :, j * LANES : (j + 1) * LANES] = rows_ref[j, pl.ds(m, strip, stride=modes), :].astype(jnp.bfloat16)


def start_kernel(strip, inv_ref, field_ref, out_ref, first_ref, unmix_ref, both_ref, rows_ref):
    apply_section(strip, inv_ref, field_ref, out_ref, unmix_ref, both_ref, rows_ref, 0)
    first_ref[...] = both_ref[0]


def apply_kernel(strip, inv_ref, field_ref, first_ref, whole_ref, out_ref, last_ref, pack_ref, unmix_ref, both_ref, rows_ref, wide_ref):
    modes = inv_ref.shape[1]
    s = pl.program_id(0)

    @pl.when(s == 0)
    def _():
        wide_ref[...] = jnp.zeros_like(wide_ref)
        pack_ref[...] = jnp.zeros_like(pack_ref)
        both_ref[0] = first_ref[...]

    slot = lax.rem(s + 1, 2)
    apply_section(strip, inv_ref, field_ref, out_ref, unmix_ref, both_ref, rows_ref, slot)
    place(dot_nt(both_ref[1 - slot], both_ref[slot]), wide_ref, pack_ref, s, modes)

    @pl.when(s == pl.num_programs(0) - 1)
    def _():
        last_ref[...] = both_ref[slot]


def edge_kernel(sections, pack_ref, last_ref, next_ref, out_ref, wide_ref):
    wide_ref[...] = jnp.zeros_like(wide_ref)
    out_ref[...] = pack_ref[...]
    place(dot_nt(last_ref[...], next_ref[...]), wide_ref, out_ref, jnp.int32(sections - 1), last_ref.shape[0])


def couple_kernel(columns, x_ref, out_ref, slots, send_sem, recv_sem):
    sections, modes, _ = out_ref.shape
    total = gathered_sum(x_ref, slots, send_sem, recv_sem)
    parts = spread(total, sections)
    end = lax.axis_size("sec") * sections - 1
    for s in range(sections):
        kept = jnp.where(lax.axis_index("sec") * sections + s < end, 1.0 / (columns * math.sqrt(columns)), 0.0)
        out_ref[s] = parts[s][:, 0:modes] * kept.astype(jnp.float32)


def per_device(start_modes, permittivity, heights):
    sections, modes, strip, columns = start_modes.shape
    groups = columns // LANES
    width = STEPS * DEG
    rows = -(-(strip + 2 * width) // 16) * 16
    packs = -(-sections // PER)
    tiles = lax.axis_size("tile")
    f32, bf16 = jnp.float32, jnp.bfloat16
    perm = widened(permittivity, 1, width, rows)
    pack_shape = jax.ShapeDtypeStruct((packs, modes, LANES), f32)
    pack_spec = pl.BlockSpec((packs, modes, LANES), lambda s, *_: (0, 0, 0))
    field_shape = jax.ShapeDtypeStruct((sections, groups, strip * modes, LANES), f32)
    chunks = 2 if sections % (2 * PER) == 0 else 1
    size = sections // chunks
    pending, field, grams = start_modes, None, []
    x = widened(lax.slice_in_dim(pending, 0, size, axis=0), 2, width, rows)
    for chunk in range(chunks):
        section0 = chunk * size
        if chunk + 1 < chunks:
            x, pending = lax.optimization_barrier((x, pending))
            upcoming = widened(lax.slice_in_dim(pending, section0 + size, section0 + 2 * size, axis=0), 2, width, rows)
        count = size // PER if chunks > 1 else packs
        held = [] if field is None else [field]
        kernel = functools.partial(filter_kernel, strip, section0, sections)
        if not held:
            kernel = functools.partial(lambda inner, h, x, p, *rest: inner(h, x, p, None, *rest), kernel)
        field, gram = pl.pallas_call(
            kernel,
            grid_spec=pltpu.PrefetchScalarGridSpec(
                num_scalar_prefetch=1,
                grid=(size,),
                in_specs=[
                    pl.BlockSpec((1, modes, rows, columns), lambda s, *_: (s, 0, 0, 0)),
                    pl.BlockSpec((1, rows, columns), lambda s, *_, section0=section0: (s + section0, 0, 0)),
                ]
                + [pl.BlockSpec(memory_space=pl.ANY)] * len(held),
                out_specs=[
                    pl.BlockSpec((1, groups, strip * modes, LANES), lambda s, *_, section0=section0: (s + section0, 0, 0, 0)),
                    pl.BlockSpec((count, modes, LANES), lambda s, *_: (0, 0, 0)),
                ],
                scratch_shapes=[
                    pltpu.VMEM((groups, (rows + 2) * modes, LANES), f32),
                    pltpu.VMEM((groups, (rows + 2) * modes, LANES), f32),
                    pltpu.VMEM((groups, rows, LANES), f32),
                    pltpu.VMEM((columns, columns), bf16),
                    pltpu.VMEM((modes, strip * columns), bf16),
                    pltpu.VMEM((modes, strip * columns), bf16),
                    pltpu.VMEM((modes, LANES), f32),
                ],
            ),
            out_shape=[field_shape, jax.ShapeDtypeStruct((count, modes, LANES), f32)],
            input_output_aliases={3: 0} if held else {},
            cost_estimate=pl.CostEstimate(flops=size * 10**9, bytes_accessed=size * 2 * 10**6, transcendentals=0),
            name="filter",
        )(heights, x, perm, *held)
        grams.append(gram)
        if chunk + 1 < chunks:
            x = upcoming
    gram = jnp.concatenate(grams, axis=0) if chunks > 1 else grams[0]

    def exchanged(kernel, value, collective_id, name):
        return pl.pallas_call(
            kernel,
            out_shape=jax.ShapeDtypeStruct((sections, modes, modes), f32),
            in_specs=[pl.BlockSpec(memory_space=pltpu.VMEM)],
            out_specs=pl.BlockSpec(memory_space=pltpu.VMEM),
            scratch_shapes=[
                pltpu.VMEM((tiles, packs, modes, LANES), f32),
                pltpu.SemaphoreType.DMA((tiles,)),
                pltpu.SemaphoreType.DMA((tiles,)),
            ],
            compiler_params=pltpu.CompilerParams(collective_id=collective_id, has_side_effects=True),
            name=name,
        )(value)

    inverse = exchanged(functools.partial(factor_kernel, float(columns)), gram, 0, "factor")
    flat = jax.ShapeDtypeStruct((modes, strip * columns), bf16)
    flat_spec = pl.BlockSpec((modes, strip * columns), lambda s: (0, 0))
    scaled_shape = jax.ShapeDtypeStruct((sections, modes, strip, columns), bf16)
    work = [
        pltpu.VMEM((columns, columns), bf16),
        pltpu.VMEM((2, modes, strip * columns), bf16),
        pltpu.VMEM((groups, strip * modes, LANES), f32),
    ]

    def specs(skip):
        inverse_spec = pl.BlockSpec((1, modes, modes), lambda s: (s + skip, 0, 0))
        part = pl.BlockSpec((1, groups, strip * modes, LANES), lambda s: (s + skip, 0, 0, 0))
        return [inverse_spec, part], pl.BlockSpec((1, modes, strip, columns), lambda s: (s + skip, 0, 0, 0))

    inputs, outputs = specs(0)
    scaled, first = pl.pallas_call(
        functools.partial(start_kernel, strip),
        grid=(1,),
        in_specs=inputs,
        out_specs=[outputs, flat_spec],
        out_shape=[scaled_shape, flat],
        scratch_shapes=work,
        name="start",
    )(inverse, field)
    inputs, outputs = specs(1)
    scaled, last, pack = pl.pallas_call(
        functools.partial(apply_kernel, strip),
        grid=(sections - 1,),
        in_specs=inputs + [flat_spec, pl.BlockSpec(memory_space=pl.ANY)],
        out_specs=[outputs, flat_spec, pack_spec],
        out_shape=[scaled_shape, flat, pack_shape],
        scratch_shapes=work + [pltpu.VMEM((modes, LANES), f32)],
        input_output_aliases={3: 0},
        cost_estimate=pl.CostEstimate(flops=sections * 10**9, bytes_accessed=sections * 10**6, transcendentals=0),
        name="apply",
    )(inverse, field, first, scaled)
    count = lax.axis_size("sec")
    arriving = lax.ppermute(first, "sec", [(i + 1, i) for i in range(count - 1)])
    pack = pl.pallas_call(
        functools.partial(edge_kernel, sections),
        out_shape=pack_shape,
        scratch_shapes=[pltpu.VMEM((modes, LANES), f32)],
        name="edge",
    )(pack, last, arriving)
    coupling = exchanged(functools.partial(couple_kernel, columns), pack, 1, "couple")
    return (scaled, coupling)


def solution(mesh):
    placed = (P("sec", None, "tile", None), P("sec", "tile", None), P())
    return jax.shard_map(
        per_device,
        mesh=mesh,
        in_specs=placed,
        out_specs=(P("sec", None, "tile", None), P("sec", None, None)),
        check_vma=False,
    )
```

```python
import functools
import math

import jax
import jax.numpy as jnp
from jax import lax
from jax.experimental import pallas as pl
from jax.experimental.pallas import tpu as pltpu
from jax.sharding import PartitionSpec as P

STEPS = 3
DEG = 4
SHIFT_DIAG = 3.0
EPS_WEIGHT = 0.25
LOWER_EDGE = 2.0
UPPER_EDGE = 10.75
CENTER = 0.5 * (UPPER_EDGE + LOWER_EDGE)
RADIUS = 0.5 * (UPPER_EDGE - LOWER_EDGE)
LANES = 128
SLOT = 32
PER = LANES // SLOT
BLOCK = 8

NT = (((1,), (1,)), ((), ()))
MESH = pl.DeviceIdType.MESH


def iota(shape, dim):
    return lax.broadcasted_iota(jnp.int32, shape, dim)


def dot32(a, b):
    return jnp.dot(a, b, preferred_element_type=jnp.float32)


def dot_nt(a, b):
    return lax.dot_general(a, b, NT, preferred_element_type=jnp.float32)


def halo(x, dim, width):
    size, strip = lax.axis_size("tile"), x.shape[dim]
    above, below = [], []
    for hop in range(1, -(-width // strip) + 1):
        rows = min(strip, width - (hop - 1) * strip)
        last = lax.slice_in_dim(x, strip - rows, strip, axis=dim)
        first = lax.slice_in_dim(x, 0, rows, axis=dim)
        above.insert(0, lax.ppermute(last, "tile", [(i, i + hop) for i in range(size - hop)]))
        below.append(lax.ppermute(first, "tile", [(i + hop, i) for i in range(size - hop)]))
    return above, below


def widened(x, dim, width, total):
    above, below = halo(x, dim, width)
    spare = total - x.shape[dim] - 2 * width
    parts = above + [x] + below
    if spare:
        shape = list(x.shape)
        shape[dim] = spare
        parts.append(jnp.zeros(shape, x.dtype))
    return jnp.concatenate(parts, axis=dim)


def interleave(columns, groups, inverse=False):
    row, col = iota((columns, columns), 0), iota((columns, columns), 1)
    if inverse:
        row, col = col, row
    return (row == groups * (col % LANES) + col // LANES).astype(jnp.bfloat16)


def place(small, wide_ref, out_ref, s, modes):
    wide_ref[:, 0:modes] = small
    moved = pltpu.roll(wide_ref[...], SLOT * lax.rem(s, PER), 1)
    group = s // PER
    out_ref[group] = out_ref[group] + moved


def filter_kernel(strip, section0, sections, heights, x_ref, perm_ref, whole_ref, field_ref, gram_ref, a_ref, b_ref, q_ref, mix_ref, high_ref, low_ref, wide_ref):
    modes, rows, columns = x_ref.shape[1:]
    groups = columns // LANES
    width = STEPS * DEG
    used = strip + 2 * width
    s = pl.program_id(0)
    height = heights[lax.axis_index("sec") * sections + section0 + s]
    top = lax.axis_index("tile") * strip - width

    @pl.when(s == 0)
    def _():
        mix_ref[...] = interleave(columns, groups)
        a_ref[...] = jnp.zeros_like(a_ref)
        b_ref[...] = jnp.zeros_like(b_ref)
        wide_ref[...] = jnp.zeros_like(wide_ref)
        gram_ref[...] = jnp.zeros_like(gram_ref)

    mix = mix_ref[...]
    row_ids = top + iota((rows, LANES), 0)
    valid = (row_ids >= 0) & (row_ids < height)
    batch = 4
    for m0 in range(0, modes, batch):
        moved = dot32(x_ref[0, m0 : m0 + batch].reshape(batch * rows, columns), mix)
        for m in range(batch):
            for j in range(groups):
                value = moved[m * rows : (m + 1) * rows, j * LANES : (j + 1) * LANES]
                a_ref[j, pl.ds(modes + m0 + m, rows, stride=modes), :] = jnp.where(valid, value, 0.0)
    perm = dot32(perm_ref[0], mix)
    diag = (4.0 + SHIFT_DIAG - EPS_WEIGHT * perm - CENTER) * (2.0 / RADIUS)
    for j in range(groups):
        q_ref[j] = diag[:, j * LANES : (j + 1) * LANES]

    lane = iota((8, LANES), 1)
    is_first, is_last = lane == 0, lane == LANES - 1

    def stage(src, dst, order, start):
        blocks = -(-(used - 2 * order) // BLOCK)
        low = min(order, rows - blocks * BLOCK)

        def body(block, carry):
            row0 = low + block * BLOCK
            base = pl.multiple_of((row0 + 1) * modes, 8)
            for tile in range(modes // 8):
                def load(ref, i, j):
                    return ref[j, pl.ds(pl.multiple_of(base + (i * modes + tile * 8), 8), 8), :]

                before = [load(src, -1, j) for j in range(groups)]
                here = [load(src, 0, j) for j in range(groups)]
                for i in range(BLOCK):
                    after = [load(src, i + 1, j) for j in range(groups)]
                    row = top + row0 + i
                    inside = (row >= 0) & (row < height)
                    weight = jnp.where(inside, 2.0 / RADIUS, 0.0).astype(jnp.float32)
                    left = jnp.where(is_first, 0.0, pltpu.roll(here[groups - 1], 1, 1))
                    right = jnp.where(is_last, 0.0, pltpu.roll(here[0], LANES - 1, 1))
                    for j in range(groups):
                        side = (here[j - 1] if j else left) + (here[j + 1] if j < groups - 1 else right)
                        beside = (before[j] + after[j]) + side
                        q = jnp.broadcast_to(q_ref[j, pl.ds(row0 + i, 1), :], (8, LANES))
                        value = q * here[j] - weight * beside
                        if start:
                            value = 0.5 * value
                        else:
                            value = value - load(dst, i, j)
                        dst[j, pl.ds(pl.multiple_of(base + (i * modes + tile * 8), 8), 8), :] = value
                    before, here = here, after
            return carry

        lax.fori_loop(0, blocks, body, 0)

    for step in range(STEPS):
        for k in range(DEG):
            src, dst = (a_ref, b_ref) if k % 2 == 0 else (b_ref, a_ref)
            stage(src, dst, step * DEG + k + 1, k == 0)

    for j in range(groups):
        field_ref[0, j] = a_ref[j, (width + 1) * modes : (width + 1 + strip) * modes, :]
    for r in range(strip):
        for j in range(groups):
            value = a_ref[j, (width + 1 + r) * modes : (width + 2 + r) * modes, :]
            high = value.astype(jnp.bfloat16)
            place_at = slice((r * groups + j) * LANES, (r * groups + j + 1) * LANES)
            high_ref[:, place_at] = high
            low_ref[:, place_at] = (value - high.astype(jnp.float32)).astype(jnp.bfloat16)
    high, low = high_ref[...], low_ref[...]
    gram = dot_nt(high, high) + (dot_nt(high, low) + dot_nt(low, high))
    place(gram, wide_ref, gram_ref, s, modes)


def rounds_of(count):
    return count.bit_length() - 1 if count & (count - 1) == 0 else 0


def summed(x_ref, slots, sums, send_sem, recv_sem):
    rounds = rounds_of(lax.axis_size("tile"))
    if not rounds:
        return gathered_sum(x_ref, slots, send_sem, recv_sem)
    me = lax.axis_index("tile")
    peers = [me + (1 << k) * (1 - 2 * lax.rem(me // (1 << k), 2)) for k in range(rounds)]
    barrier = pltpu.get_barrier_semaphore()
    for peer in peers:
        pl.semaphore_signal(barrier, inc=1, device_id={"tile": peer}, device_id_type=MESH)
    pl.semaphore_wait(barrier, rounds)
    copies = []
    for k, peer in enumerate(peers):
        source = sums.at[k - 1] if k else x_ref
        copy = pltpu.make_async_remote_copy(
            src_ref=source,
            dst_ref=slots.at[k],
            send_sem=send_sem.at[k],
            recv_sem=recv_sem.at[k],
            device_id={"tile": peer},
            device_id_type=MESH,
        )
        copy.start()
        copies.append(copy)
        copy.wait_recv()
        total = source[...] + slots[k]
        if k < rounds - 1:
            sums[k] = total
    for copy in copies:
        copy.wait_send()
    return total


def gathered_sum(x_ref, slots, send_sem, recv_sem):
    count = lax.axis_size("tile")
    me = lax.axis_index("tile")
    barrier = pltpu.get_barrier_semaphore()

    def greet(d, carry):
        pl.semaphore_signal(barrier, inc=1, device_id={"tile": lax.rem(me + d, count)}, device_id_type=MESH)
        return carry

    lax.fori_loop(1, count, greet, 0)
    pl.semaphore_wait(barrier, count - 1)

    def copy_to(d, slot):
        return pltpu.make_async_remote_copy(
            src_ref=x_ref,
            dst_ref=slots.at[slot],
            send_sem=send_sem.at[d],
            recv_sem=recv_sem.at[slot],
            device_id={"tile": lax.rem(me + d, count)},
            device_id_type=MESH,
        )

    def send(d, carry):
        copy_to(d, me).start()
        return carry

    def finish(d, carry):
        copy_to(d, lax.rem(me + count - d, count)).wait_recv()
        copy_to(d, me).wait_send()
        return carry

    lax.fori_loop(1, count, send, 0)
    slots[me] = x_ref[...]
    lax.fori_loop(1, count, finish, 0)
    return lax.fori_loop(1, count, lambda i, total: total + slots[i], slots[0])


def spread(total, sections):
    return jnp.stack([pltpu.roll(total[s // PER], (LANES - SLOT * (s % PER)) % LANES, 1) if s % PER else total[s // PER] for s in range(sections)])


def factor_kernel(scale, x_ref, out_ref, slots, sums, send_sem, recv_sem):
    sections, modes, _ = out_ref.shape
    total = summed(x_ref, slots, sums, send_sem, recv_sem)
    shape = (sections, modes, LANES)
    row, lane = iota(shape, 1), iota(shape, 2)
    work = jnp.where(lane < modes, spread(total, sections), jnp.where(lane == row + SLOT, 1.0, 0.0))
    pivots = jnp.ones((sections, modes, 1), jnp.float32)
    for k in range(modes):
        top = work[:, k : k + 1, :]
        pivot = work[:, k : k + 1, k : k + 1]
        pivots = jnp.where(row[:, :, 0:1] == k, pivot, pivots)
        if k < modes - 1:
            column = jnp.where(row > k, work[:, :, k : k + 1], 0.0)
            work = work - column * (top * (1.0 / pivot))
    work = work * (scale / jnp.sqrt(pivots))
    for s in range(sections):
        moved = pltpu.roll(work[s], LANES - SLOT, 1)
        out_ref[s] = moved[:, 0:modes]


def apply_section(strip, inv_ref, field_ref, out_ref, unmix_ref, both_ref, rows_ref, slot):
    modes = inv_ref.shape[1]
    groups = field_ref.shape[1]
    columns = groups * LANES
    take = max(n for n in range(1, 9) if strip % n == 0)
    size = take * modes


    @pl.when(pl.program_id(0) == 0)
    def _():
        unmix_ref[...] = interleave(columns, groups, True)

    copies = (iota((size, modes), 0) % modes == iota((size, modes), 1)).astype(jnp.bfloat16)
    same = iota((size, size), 0) // modes == iota((size, size), 1) // modes

    def block_diagonal(part):
        tall = dot32(copies, part).astype(jnp.bfloat16)
        return jnp.where(same, dot_nt(tall, copies), 0.0).astype(jnp.bfloat16)

    inv = inv_ref[0]
    inv_high = inv.astype(jnp.bfloat16)
    inv_low = (inv - inv_high.astype(jnp.float32)).astype(jnp.bfloat16)
    left_high, left_low = block_diagonal(inv_high), block_diagonal(inv_low)
    unmix = unmix_ref[...]
    for r0 in range(0, strip, take):
        value = jnp.concatenate([field_ref[0, j, r0 * modes : r0 * modes + size, :] for j in range(groups)], axis=1)
        high = value.astype(jnp.bfloat16)
        low = (value - high.astype(jnp.float32)).astype(jnp.bfloat16)
        solved = dot32(left_high, high) + (dot32(left_low, high) + dot32(left_high, low))
        for r in range(take):
            both_ref[slot, :, (r0 + r) * columns : (r0 + r + 1) * columns] = solved[r * modes : (r + 1) * modes].astype(jnp.bfloat16)
        natural = dot32(solved.astype(jnp.bfloat16), unmix)
        for j in range(groups):
            rows_ref[j, r0 * modes : r0 * modes + size, :] = natural[:, j * LANES : (j + 1) * LANES]
    for m in range(modes):
        for j in range(groups):
            out_ref[0, m, :, j * LANES : (j + 1) * LANES] = rows_ref[j, pl.ds(m, strip, stride=modes), :].astype(jnp.bfloat16)


def start_kernel(strip, inv_ref, field_ref, out_ref, first_ref, unmix_ref, both_ref, rows_ref):
    apply_section(strip, inv_ref, field_ref, out_ref, unmix_ref, both_ref, rows_ref, 0)
    first_ref[...] = both_ref[0]


def apply_kernel(strip, inv_ref, field_ref, first_ref, whole_ref, out_ref, last_ref, pack_ref, unmix_ref, both_ref, rows_ref, wide_ref):
    modes = inv_ref.shape[1]
    s = pl.program_id(0)

    @pl.when(s == 0)
    def _():
        wide_ref[...] = jnp.zeros_like(wide_ref)
        pack_ref[...] = jnp.zeros_like(pack_ref)
        both_ref[0] = first_ref[...]

    slot = lax.rem(s + 1, 2)
    apply_section(strip, inv_ref, field_ref, out_ref, unmix_ref, both_ref, rows_ref, slot)
    place(dot_nt(both_ref[1 - slot], both_ref[slot]), wide_ref, pack_ref, s, modes)

    @pl.when(s == pl.num_programs(0) - 1)
    def _():
        last_ref[...] = both_ref[slot]


def edge_kernel(sections, pack_ref, last_ref, next_ref, out_ref, wide_ref):
    wide_ref[...] = jnp.zeros_like(wide_ref)
    out_ref[...] = pack_ref[...]
    place(dot_nt(last_ref[...], next_ref[...]), wide_ref, out_ref, jnp.int32(sections - 1), last_ref.shape[0])


def couple_kernel(columns, x_ref, out_ref, slots, sums, send_sem, recv_sem):
    sections, modes, _ = out_ref.shape
    total = summed(x_ref, slots, sums, send_sem, recv_sem)
    parts = spread(total, sections)
    end = lax.axis_size("sec") * sections - 1
    for s in range(sections):
        kept = jnp.where(lax.axis_index("sec") * sections + s < end, 1.0 / (columns * math.sqrt(columns)), 0.0)
        out_ref[s] = parts[s][:, 0:modes] * kept.astype(jnp.float32)


def per_device(start_modes, permittivity, heights):
    sections, modes, strip, columns = start_modes.shape
    groups = columns // LANES
    width = STEPS * DEG
    rows = -(-(strip + 2 * width) // 16) * 16
    packs = -(-sections // PER)
    tiles = lax.axis_size("tile")
    slots = rounds_of(tiles) or tiles
    f32, bf16 = jnp.float32, jnp.bfloat16
    perm = widened(permittivity, 1, width, rows)
    pack_shape = jax.ShapeDtypeStruct((packs, modes, LANES), f32)
    pack_spec = pl.BlockSpec((packs, modes, LANES), lambda s, *_: (0, 0, 0))
    field_shape = jax.ShapeDtypeStruct((sections, groups, strip * modes, LANES), f32)
    chunks = 2 if sections % (2 * PER) == 0 else 1
    size = sections // chunks
    pending, field, grams = start_modes, None, []
    x = widened(lax.slice_in_dim(pending, 0, size, axis=0), 2, width, rows)
    for chunk in range(chunks):
        section0 = chunk * size
        if chunk + 1 < chunks:
            x, perm, pending = lax.optimization_barrier((x, perm, pending))
            upcoming = widened(lax.slice_in_dim(pending, section0 + size, section0 + 2 * size, axis=0), 2, width, rows)
        count = size // PER if chunks > 1 else packs
        held = [] if field is None else [field]
        kernel = functools.partial(filter_kernel, strip, section0, sections)
        if not held:
            kernel = functools.partial(lambda inner, h, x, p, *rest: inner(h, x, p, None, *rest), kernel)
        field, gram = pl.pallas_call(
            kernel,
            grid_spec=pltpu.PrefetchScalarGridSpec(
                num_scalar_prefetch=1,
                grid=(size,),
                in_specs=[
                    pl.BlockSpec((1, modes, rows, columns), lambda s, *_: (s, 0, 0, 0)),
                    pl.BlockSpec((1, rows, columns), lambda s, *_, section0=section0: (s + section0, 0, 0)),
                ]
                + [pl.BlockSpec(memory_space=pl.ANY)] * len(held),
                out_specs=[
                    pl.BlockSpec((1, groups, strip * modes, LANES), lambda s, *_, section0=section0: (s + section0, 0, 0, 0)),
                    pl.BlockSpec((count, modes, LANES), lambda s, *_: (0, 0, 0)),
                ],
                scratch_shapes=[
                    pltpu.VMEM((groups, (rows + 2) * modes, LANES), f32),
                    pltpu.VMEM((groups, (rows + 2) * modes, LANES), f32),
                    pltpu.VMEM((groups, rows, LANES), f32),
                    pltpu.VMEM((columns, columns), bf16),
                    pltpu.VMEM((modes, strip * columns), bf16),
                    pltpu.VMEM((modes, strip * columns), bf16),
                    pltpu.VMEM((modes, LANES), f32),
                ],
            ),
            out_shape=[field_shape, jax.ShapeDtypeStruct((count, modes, LANES), f32)],
            input_output_aliases={3: 0} if held else {},
            cost_estimate=pl.CostEstimate(flops=size * 10**9, bytes_accessed=size * 2 * 10**6, transcendentals=0),
            name="filter",
        )(heights, x, perm, *held)
        grams.append(gram)
        if chunk + 1 < chunks:
            x = upcoming
    gram = jnp.concatenate(grams, axis=0) if chunks > 1 else grams[0]

    def exchanged(kernel, value, collective_id, name):
        return pl.pallas_call(
            kernel,
            out_shape=jax.ShapeDtypeStruct((sections, modes, modes), f32),
            in_specs=[pl.BlockSpec(memory_space=pltpu.VMEM)],
            out_specs=pl.BlockSpec(memory_space=pltpu.VMEM),
            scratch_shapes=[
                pltpu.VMEM((slots, packs, modes, LANES), f32),
                pltpu.VMEM((slots, packs, modes, LANES), f32),
                pltpu.SemaphoreType.DMA((slots,)),
                pltpu.SemaphoreType.DMA((slots,)),
            ],
            compiler_params=pltpu.CompilerParams(collective_id=collective_id, has_side_effects=True),
            name=name,
        )(value)

    inverse = exchanged(functools.partial(factor_kernel, float(columns)), gram, 0, "factor")
    flat = jax.ShapeDtypeStruct((modes, strip * columns), bf16)
    flat_spec = pl.BlockSpec((modes, strip * columns), lambda s: (0, 0))
    scaled_shape = jax.ShapeDtypeStruct((sections, modes, strip, columns), bf16)
    work = [
        pltpu.VMEM((columns, columns), bf16),
        pltpu.VMEM((2, modes, strip * columns), bf16),
        pltpu.VMEM((groups, strip * modes, LANES), f32),
    ]

    def specs(skip):
        inverse_spec = pl.BlockSpec((1, modes, modes), lambda s: (s + skip, 0, 0))
        part = pl.BlockSpec((1, groups, strip * modes, LANES), lambda s: (s + skip, 0, 0, 0))
        return [inverse_spec, part], pl.BlockSpec((1, modes, strip, columns), lambda s: (s + skip, 0, 0, 0))

    inputs, outputs = specs(0)
    scaled, first = pl.pallas_call(
        functools.partial(start_kernel, strip),
        grid=(1,),
        in_specs=inputs,
        out_specs=[outputs, flat_spec],
        out_shape=[scaled_shape, flat],
        scratch_shapes=work,
        name="start",
    )(inverse, field)
    inputs, outputs = specs(1)
    scaled, last, pack = pl.pallas_call(
        functools.partial(apply_kernel, strip),
        grid=(sections - 1,),
        in_specs=inputs + [flat_spec, pl.BlockSpec(memory_space=pl.ANY)],
        out_specs=[outputs, flat_spec, pack_spec],
        out_shape=[scaled_shape, flat, pack_shape],
        scratch_shapes=work + [pltpu.VMEM((modes, LANES), f32)],
        input_output_aliases={3: 0},
        cost_estimate=pl.CostEstimate(flops=sections * 10**9, bytes_accessed=sections * 10**6, transcendentals=0),
        name="apply",
    )(inverse, field, first, scaled)
    count = lax.axis_size("sec")
    arriving = lax.ppermute(first, "sec", [(i + 1, i) for i in range(count - 1)])
    pack = pl.pallas_call(
        functools.partial(edge_kernel, sections),
        out_shape=pack_shape,
        scratch_shapes=[pltpu.VMEM((modes, LANES), f32)],
        name="edge",
    )(pack, last, arriving)
    coupling = exchanged(functools.partial(couple_kernel, columns), pack, 1, "couple")
    return (scaled, coupling)


def solution(mesh):
    placed = (P("sec", None, "tile", None), P("sec", "tile", None), P())
    return jax.shard_map(
        per_device,
        mesh=mesh,
        in_specs=placed,
        out_specs=(P("sec", None, "tile", None), P("sec", None, None)),
        check_vma=False,
    )
```
